128 devices in a mesh: tok: 8 (over x, z_lo), blk: 16 (over z_hi, y, core).
Axes of the slice: x: 4, y: 4, z: 4 (z_hi: 2, z_lo: 2; z = z_hi * 2 + z_lo), core: 2. Of those that a mesh axis runs over, the one named last changes fastest.
Arguments:
- states: bfloat16 [48, 512, 1024], P('blk', 'tok'), may hold values from -6 to 6
- gain_attn: bfloat16 [1024], replicated, may hold values from 0.099609375 to 1.8984375
- w_qkv: bfloat16 [1024, 3072], replicated, may hold values from -4 to 4
- w_out: bfloat16 [1024, 1024], replicated, may hold values from -0.1875 to 0.1875
- cache_prev: bfloat16 [48, 1536, 2, 1024], P('blk', 'tok'), may hold values from -6 to 6
- cached_blocks: int32 [48], P('blk'), may hold values from 0 to 12, as said below
- gain_moe: bfloat16 [1024], replicated, may hold values from 0.099609375 to 1.8984375
- w_router: bfloat16 [1024, 16], replicated, may hold values from -0.1875 to 0.1875
- routes: int32 [8, 48, 64, 2], P('tok', 'blk'), may hold values from 0 to 15, all different within a row; in each aligned block of 192 rows (0 to 191, 192 to 383, ..., all dimensions but the last counted through in order) at most 30 rows name the same one
- w_gate_up: bfloat16 [16, 2, 1024, 2816], P('blk', None, None, 'tok'), may hold values from -0.1875 to 0.1875
- w_down: bfloat16 [16, 2816, 1024], P('blk', 'tok'), may hold values from -0.109375 to 0.109375
Outputs:
- out_hidden: bfloat16 [48, 512, 1024], P('blk', 'tok')
- decode_cache: bfloat16 [48, 2048, 2, 1024], P('blk', None, None, 'tok')
The draws below stay inside these ranges and needn't reach their ends.
Inputs may be any that keep to these rules, and one draw needn't show every extreme that they name: `cached_blocks`: some request holds all 12 blocks. `routes`: among the 192 tokens of one device, no expert is named more than 30 times.
All inputs are finite; a program needn't handle non-finite values.
Results may differ from the reference program's by a relative error of at most 0.0065.
Values may be sent and summed in bfloat16 or wider, within the bound.
A program may use at most 192 MiB of HBM per device.

```python
import math
import jax
import jax.numpy as jnp
import numpy as np
from jax import lax

D = 1024
HEADS = 16
HEAD_DIM = 64
FF = 2816
EXPERTS = 16
TOP = 2
BLOCK = 128
GROUP = 512
CACHE_BLOCKS = 12
REQS = 48
GROUP_DEV = 64
TOK_DEV = 192
CACHE_LEN = 1536
CAPACITY = 30
N_TOK = 8
N_BLK = 16


def draw_w_qkv(key, part):
    base = jax.random.normal(key, (D, 3 * D), jnp.float32) * D ** (-0.5)
    return jnp.clip(base, -4.0, 4.0).astype(jnp.bfloat16)


def draw_cached_blocks(key, part):
    first_key = jax.random.fold_in(key, 11)
    second_key = jax.random.fold_in(key, 23)
    counts = jax.random.randint(first_key, (REQS,), 0, CACHE_BLOCKS + 1)
    picked = jax.random.randint(second_key, (), 0, REQS)
    return jnp.where(jnp.arange(REQS) == picked, CACHE_BLOCKS, counts).astype(jnp.int32)


def block_scale(key, shape, cuts, least, largest):
    loudness, own = 1.0, jax.random.fold_in(key, 6)
    for axis_at, shards_of in cuts:
        heights = jnp.exp(jax.random.uniform(jax.random.fold_in(own, axis_at), (shards_of,), jnp.float32, least / len(cuts), largest / len(cuts)))
        loudness = loudness * jnp.repeat(heights, shape[axis_at] // shards_of).reshape([-1 if axis == axis_at else 1 for axis in range(len(shape))])
    return loudness


def shared_out(key, own, number, rows, count, top, reach, slope):
    order = jax.random.permutation(key, count)
    crowded, common = shares(count, rows * top, reach, slope, True), shares(count, rows * top, reach, slope, False)
    places = jnp.arange(count)

    def named(sizes, rotation):
        used = int((sizes > 0).sum())
        fixed = max(1, used // 4)
        passed = fixed + (places - fixed + rotation * (used - fixed)) % max(1, count - fixed)
        return jnp.zeros((count,), jnp.int32).at[order[jnp.where(places < fixed, places, passed)]].set(jnp.asarray(sizes, jnp.int32))

    sizes = jnp.where(number % 4 == 0, named(crowded, number // 4), named(common, number - number // 4 - 1))
    mixed = jax.random.permutation(jax.random.fold_in(own, 3), count)
    source_of, sink = mixed[0:count // 2 * 2:2], mixed[1:count // 2 * 2:2]
    room = jnp.minimum(sizes[source_of] - 1, reach - sizes[sink]) // 2
    room = jnp.where((source_of == order[0]) | (sink == order[0]) | (sizes[sink] == 0), 0, jnp.maximum(room, 0))
    passed = jax.random.randint(jax.random.fold_in(own, 4), (count // 2,), 0, 1 << 20) % (room + 1)
    sizes = sizes.at[source_of].add(-passed).at[sink].add(passed)
    members = jnp.searchsorted(jnp.cumsum(sizes), jnp.arange(rows * top), side="right").astype(jnp.int32)
    table = members.reshape(top, rows).T
    table = table[jax.random.permutation(jax.random.fold_in(own, 1), rows)]
    rotation = jax.random.randint(jax.random.fold_in(own, 2), (rows, 1), 0, top)
    return jnp.take_along_axis(table, (jnp.arange(top)[None, :] + rotation) % top, axis=1)


def shares(amount, total, bound, skew, full):
    portions = [(1 << 20) // math.isqrt(standing ** skew) + 1 for standing in range(1, amount + 1)]
    largest = bound if full else min(bound, max(-(-total // amount), total * portions[0] // sum(portions)))
    least = 1 if total - largest >= amount - 1 else 0
    given, rest = [largest] + [least] * (amount - 1), total - largest - least * (amount - 1)
    while rest > 0:
        candidates = [i for i in range(1, amount) if given[i] < largest] or [i for i in range(1, amount) if given[i] < bound]
        mass, budget = sum([portions[i] for i in candidates]), rest
        for i in candidates:
            more = min(bound - given[i], max(1, budget * portions[i] // mass), rest)
            given[i] = given[i] + more
            rest = rest - more
    return np.array(given)


def scatter_about(key, extent, deviation, most, pieces=(), held_as=jnp.bfloat16):
    values = jax.random.normal(key, extent, jnp.float32) * deviation
    if len(pieces) > 0:
        values = block_scale(key, extent, pieces, -0.22, 0.18) * values
    return jnp.clip(values, min=-most, max=most).astype(held_as)


def setup_inputs(seed: int = 0) -> dict:
    keys = jax.random.split(jax.random.key(seed), 12)
    states = scatter_about(keys[0], (REQS, GROUP, D), 1.0, 6.0, ((0, 16), (1, 8)))
    gain_attn = jnp.clip(1.0 + 0.18 * jax.random.normal(keys[1], (D,), jnp.float32), 0.099609375, 1.8984375).astype(jnp.bfloat16)
    w_qkv = draw_w_qkv(jax.random.fold_in(keys[11], 71), 0)
    w_out = scatter_about(keys[3], (D, D), D ** -0.5, 0.1875)
    cache_prev = scatter_about(keys[4], (REQS, CACHE_LEN, 2, D), 1.0, 6.0, ((0, 16), (1, 8)))
    cached_blocks = draw_cached_blocks(jax.random.fold_in(keys[11], 71), 0)
    gain_moe = jnp.clip(1.0 + 0.18 * jax.random.normal(keys[6], (D,), jnp.float32), 0.099609375, 1.8984375).astype(jnp.bfloat16)
    w_router = scatter_about(keys[7], (D, EXPERTS), D ** -0.5, 0.1875)
    routes_keys = jax.random.split(jax.random.fold_in(keys[8], 1), N_TOK * REQS * GROUP_DEV // TOK_DEV)
    routes_turns = jax.random.permutation(jax.random.fold_in(keys[8], 3), N_TOK * REQS * GROUP_DEV // TOK_DEV)
    routes = jax.vmap(lambda own, number: shared_out(jax.random.fold_in(keys[8], 2), own, number, TOK_DEV, EXPERTS, TOP, CAPACITY, 2))(routes_keys, routes_turns).reshape((N_TOK, REQS, GROUP_DEV, TOP))
    w_gate_up = scatter_about(keys[9], (EXPERTS, 2, D, FF), D ** -0.5, 0.1875, ((0, 16), (3, 8)))
    w_down = scatter_about(keys[10], (EXPERTS, FF, D), FF ** -0.5, 0.109375, ((0, 16), (1, 8)))
    return {"states": states, "gain_attn": gain_attn, "w_qkv": w_qkv, "w_out": w_out, "cache_prev": cache_prev, "cached_blocks": cached_blocks, "gain_moe": gain_moe, "w_router": w_router, "routes": routes, "w_gate_up": w_gate_up, "w_down": w_down}


def normalize(values, gain):
    return values * lax.rsqrt(lax.optimization_barrier(jnp.mean(values * values, -1, keepdims=True)) + 1e-06) * gain.astype(jnp.float32)

def reference(states, gain_attn, w_qkv, w_out, cache_prev, cached_blocks, gain_moe, w_router, routes, w_gate_up, w_down):
    flat_states = states.reshape(REQS * GROUP, D).astype(jnp.float32)
    normed = normalize(flat_states, gain_attn).astype(jnp.bfloat16)
    projected = jnp.dot(normed, w_qkv, preferred_element_type=jnp.float32).astype(jnp.bfloat16)
    projected = projected.reshape(REQS, GROUP, 3, HEADS, HEAD_DIM)
    lengths = (cached_blocks * BLOCK).astype(jnp.int32)

    def one_request(inputs):
        fresh, cached, length = inputs
        old_heads = cached.reshape(CACHE_LEN, 2, HEADS, HEAD_DIM)
        query = fresh[:, 0].astype(jnp.float32)
        key_all = jnp.concatenate([old_heads[:, 0], fresh[:, 1]], axis=0).astype(jnp.float32)
        value_all = jnp.concatenate([old_heads[:, 1], fresh[:, 2]], axis=0).astype(jnp.float32)
        scores = jnp.einsum('qhd,khd->hqk', query, key_all) * HEAD_DIM ** (-0.5)
        key_pos = jnp.arange(CACHE_LEN + GROUP)
        query_pos = jnp.arange(GROUP)
        valid = jnp.where(key_pos[None, :] < CACHE_LEN, key_pos[None, :] < length, key_pos[None, :] - CACHE_LEN <= query_pos[:, None])
        scores = jnp.where(valid[None], scores, -1e+30)
        highest = lax.optimization_barrier(jnp.max(scores, axis=-1, keepdims=True))
        weights = jnp.exp(scores - highest)
        weights = (weights / lax.optimization_barrier(jnp.sum(weights, axis=-1, keepdims=True))).astype(jnp.bfloat16)
        attended = jnp.einsum('hqk,khd->qhd', weights.astype(jnp.float32), value_all).astype(jnp.bfloat16).reshape(GROUP, D)
        keep = jnp.arange(CACHE_LEN)[:, None, None] < length
        base = jnp.concatenate([jnp.where(keep, cached, jnp.zeros((), jnp.bfloat16)), jnp.zeros((GROUP, 2, D), jnp.bfloat16)], axis=0)
        new_rows = fresh[:, 1:3].reshape(GROUP, 2, D)
        cache_out = lax.dynamic_update_slice(base, new_rows, (length, length * 0, length * 0))
        return (attended, cache_out)
    attended, decode_cache = lax.map(one_request, (projected, cache_prev, lengths))
    residual = flat_states + jnp.dot(attended.reshape(REQS * GROUP, D), w_out, preferred_element_type=jnp.float32)
    normed_moe = normalize(residual, gain_moe).astype(jnp.bfloat16)
    logits = jnp.dot(normed_moe, w_router, preferred_element_type=jnp.float32)
    route_full = jnp.transpose(routes, (1, 0, 2, 3)).reshape(REQS * GROUP, TOP)
    chosen = lax.optimization_barrier(jnp.sum(jnp.where(route_full[:, :, None] == jnp.arange(EXPERTS)[None, None, :], logits[:, None, :], 0.0), axis=-1))
    gates = jax.nn.sigmoid(chosen)
    assigned = route_full.reshape(-1)
    total_rows = REQS * GROUP * TOP
    padded = jnp.concatenate([normed_moe, jnp.zeros((1, D), jnp.bfloat16)], axis=0)
    slot_rows = N_TOK * N_BLK * CAPACITY

    def one_expert(collected, expert):
        chosen_rows = jnp.nonzero(assigned == expert, size=slot_rows, fill_value=total_rows)[0].astype(jnp.int32)
        token_rows = jnp.where(chosen_rows < total_rows, chosen_rows // TOP, REQS * GROUP).astype(jnp.int32)
        rows_in = padded[token_rows]
        gate_part = jnp.dot(rows_in, w_gate_up[expert, 0], preferred_element_type=jnp.float32)
        up_part = jnp.dot(rows_in, w_gate_up[expert, 1], preferred_element_type=jnp.float32)
        hidden = (jax.nn.gelu(gate_part, approximate=True) * up_part).astype(jnp.bfloat16)
        result = jnp.dot(hidden, w_down[expert], preferred_element_type=jnp.float32).astype(jnp.bfloat16)
        return (collected.at[chosen_rows].set(result, mode='drop'), None)
    collected = lax.scan(one_expert, jnp.zeros((total_rows, D), jnp.bfloat16), jnp.arange(EXPERTS, dtype=jnp.int32))[0]
    mixed = lax.optimization_barrier(jnp.sum(collected.reshape(REQS * GROUP, TOP, D).astype(jnp.float32) * gates[:, :, None], axis=1))
    out_hidden = (residual + mixed).astype(jnp.bfloat16).reshape(REQS, GROUP, D)
    return (out_hidden, decode_cache)
```

```python
import jax
import jax.numpy as jnp
from jax import lax
from jax.experimental import pallas as pl
from jax.experimental.pallas import tpu as pltpu
from jax.sharding import PartitionSpec as P

MESH = pl.DeviceIdType.MESH
F32, BF16 = jnp.float32, jnp.bfloat16
NT = (((1,), (1,)), ((), ()))
TN = (((0,), (0,)), ((), ()))
REQ, PER, D = 3, 64, 1024
TOK = REQ * PER
N_TOK, N_BLK, N_X = 8, 16, 4
PEERS = 2 * N_BLK
SLOTS = 32
CACHE, NEW = 1536, 512
PART = CACHE // N_TOK
FFS = 352
QROWS = 256
CHUNK = 256
LANES = 128


def normed_of(values, gain):
    return values * lax.rsqrt(jnp.mean(values * values, -1, keepdims=True) + 1e-06) * gain


def layer_kernel(
    blocks,
    states,
    gains,
    routes,
    router,
    w_qkv,
    w_out,
    cache,
    w_gu,
    w_dn,
    out,
    cache_out,
    kv_out,
    wqkv,
    wout,
    cbuf,
    qs,
    qr,
    kbuf,
    vbuf,
    wide,
    asend,
    arecv,
    resid,
    place0,
    place1,
    dsend,
    drecv,
    wg,
    wd,
    acc,
    rsend,
    rrecv,
    local,
    cache_s,
    cache_r,
    cache_l,
    qkv_s,
    qkv_r,
    att_s,
    att_r,
    att_l,
    own_s,
    own_r,
    fwd_s,
    fwd_r,
    disp_s,
    disp_r,
    ret_s,
    ret_r,
):
    me = lax.axis_index("tok")
    mb = lax.axis_index("blk")
    mx, mz = me // 2, me % 2
    mine = mz * N_BLK + mb
    right = ((mx + 1) % N_X) * 2 + mz
    left = ((mx + N_X - 1) % N_X) * 2 + mz

    def remote(src, dst, ssem, rsem, **where):
        return pltpu.make_async_remote_copy(
            src_ref=src,
            dst_ref=dst,
            send_sem=ssem,
            recv_sem=rsem,
            device_id=where,
            device_id_type=MESH,
        )

    def lanes(t):
        return pl.ds(pl.multiple_of(t * LANES, LANES), LANES)

    barrier = pltpu.get_barrier_semaphore()
    for d in range(1, N_TOK):
        pl.semaphore_signal(
            barrier, inc=1, device_id={"tok": (me + d) % N_TOK}, device_id_type=MESH
        )

    def greet(d, carry):
        j = (mine + d) % PEERS
        pl.semaphore_signal(
            barrier,
            inc=1,
            device_id={"tok": mx * 2 + j // N_BLK, "blk": j % N_BLK},
            device_id_type=MESH,
        )
        return carry

    lax.fori_loop(1, PEERS, greet, 0)

    load_qkv = pltpu.make_async_copy(w_qkv, wqkv, local.at[0])
    load_out = pltpu.make_async_copy(w_out, wout, local.at[1])
    load_gu = pltpu.make_async_copy(w_gu, wg.at[0], local.at[2])
    load_dn = pltpu.make_async_copy(w_dn, wd.at[0], local.at[3])
    load_qkv.start()
    pl.semaphore_wait(barrier, N_TOK - 1 + PEERS - 1)

    def cache_copy(r, d):
        t = (me + d) % N_TOK
        return remote(
            cache.at[r, :, :, lanes(t)],
            cbuf.at[r, me],
            cache_s.at[r, d],
            cache_r.at[r, d],
            tok=t,
        )

    def cache_own(r):
        return pltpu.make_async_copy(cache.at[r, :, :, lanes(me)], cbuf.at[r, me], cache_l.at[r])

    def send_cache(r):
        cache_own(r).start()
        for d in range(1, N_TOK):
            cache_copy(r, d).start()

    send_cache(0)
    load_out.start()
    load_gu.start()
    load_dn.start()

    with jax.named_scope("project"):
        flat = states[...].astype(F32)
        normed = normed_of(flat, gains[0:1, :]).astype(BF16)
        load_qkv.wait()
        for c in range(12):
            part = jnp.dot(
                normed, wqkv[:, c * 256 : (c + 1) * 256], preferred_element_type=F32
            ).astype(BF16)
            j, t = c // 4, (c % 4) * 2
            for half in range(2):
                qs[t + half, j * REQ : (j + 1) * REQ] = part[
                    :, half * LANES : (half + 1) * LANES
                ].reshape(REQ, PER, LANES)

    def qkv_copy(d):
        t = (me + d) % N_TOK
        return remote(qs.at[t], qr.at[:, me], qkv_s.at[d], qkv_r.at[d], tok=t)

    qkv_own = pltpu.make_async_copy(qs.at[me], qr.at[:, me], local.at[4])
    qkv_own.start()
    for d in range(1, N_TOK):
        qkv_copy(d).start()
    send_cache(1)
    send_cache(2)

    def chunk_of(ref_g, ref_d, c, lo, rows):
        if c < 2:
            return ref_g.at[pl.ds(c * FFS + lo, rows)]
        return ref_d.at[pl.ds(lo, rows)]

    def own_copy(c, side):
        return remote(
            chunk_of(w_gu, w_dn, c, 0, FFS),
            chunk_of(wg.at[1 + side], wd.at[1 + side], c, 0, FFS),
            own_s.at[c, side],
            own_r.at[c, side],
            tok=right if side == 0 else left,
        )

    def fwd_copy(c, side):
        lo = side * (FFS // 2)
        return remote(
            chunk_of(wg.at[1 + side], wd.at[1 + side], c, lo, FFS // 2),
            chunk_of(wg.at[3], wd.at[3], c, lo, FFS // 2),
            fwd_s.at[c, side],
            fwd_r.at[c, side],
            tok=right if side == 0 else left,
        )

    def send_own(c):
        for side in range(2):
            own_copy(c, side).start()

    def forward(c):
        for side in range(2):
            own_copy(c, side).wait_recv()
            fwd_copy(c, side).start()

    send_own(0)

    with jax.named_scope("places"):
        r0, r1 = routes[0:1, :], routes[1:2, :]
        expert = lax.broadcasted_iota(jnp.int32, (N_BLK, TOK), 0)
        hot0 = (expert == r0).astype(F32)
        hot1 = (expert == r1).astype(F32)
        earlier = (
            lax.broadcasted_iota(jnp.int32, (TOK, TOK), 0)
            < lax.broadcasted_iota(jnp.int32, (TOK, TOK), 1)
        ).astype(BF16)
        before0 = jnp.dot(hot0.astype(BF16), earlier, preferred_element_type=F32)
        before1 = jnp.dot(hot1.astype(BF16), earlier, preferred_element_type=F32)
        before1 = before1 + jnp.sum(hot0, axis=1, keepdims=True)
        rank0 = jnp.sum(before0 * hot0, axis=0, keepdims=True).astype(jnp.int32)
        rank1 = jnp.sum(before1 * hot1, axis=0, keepdims=True).astype(jnp.int32)
        slot = lax.broadcasted_iota(jnp.int32, (N_BLK * SLOTS, TOK), 0)
        place0[...] = (slot == r0 * SLOTS + rank0).astype(F32).astype(BF16)
        place1[...] = (slot == r1 * SLOTS + rank1).astype(F32).astype(BF16)

    qkv_own.wait()
    for d in range(1, N_TOK):
        s = (me + N_TOK - d) % N_TOK
        remote(qs.at[s], qr.at[:, s], qkv_s.at[d], qkv_r.at[d], tok=s).wait_recv()

    low_head = lax.broadcasted_iota(jnp.int32, (QROWS, LANES), 1) < LANES // 2

    def att_copy(r, d):
        t = (me + d) % N_TOK
        return remote(
            asend.at[t, r],
            arecv.at[pl.ds(pl.multiple_of(r * PER, PER), PER), lanes(me)],
            att_s.at[r, d],
            att_r.at[r, d],
            tok=t,
        )

    def att_own(r):
        return pltpu.make_async_copy(
            asend.at[me, r],
            arecv.at[pl.ds(pl.multiple_of(r * PER, PER), PER), lanes(me)],
            att_l.at[r],
        )

    def one_request(r, carry):
        cache_own(r).wait()
        for d in range(1, N_TOK):
            s = (me + N_TOK - d) % N_TOK
            remote(
                cache.at[r, :, :, lanes(s)], cbuf.at[r, s], cache_s.at[r, d], cache_r.at[r, d], tok=s
            ).wait_recv()

        def split(s, inner):
            wide[...] = cbuf.at[r, s].reshape(2 * PART, LANES)[...].astype(F32)
            rows = pl.ds(pl.multiple_of(s * PART, PART), PART)
            kbuf[rows, :] = wide[pl.ds(0, PART, stride=2), :].astype(BF16)
            vbuf[rows, :] = wide[pl.ds(1, PART, stride=2), :].astype(BF16)
            return inner

        lax.fori_loop(0, N_TOK, split, 0)
        kbuf[CACHE:, :] = qr[REQ + r].reshape(NEW, LANES)
        vbuf[CACHE:, :] = qr[2 * REQ + r].reshape(NEW, LANES)
        length = blocks[r] * LANES
        old_bias = jnp.where(
            lax.broadcasted_iota(jnp.int32, (1, CACHE), 1) < length, 0.0, -1e30
        )
        for b in range(NEW // QROWS):
            keys = (b + 1) * QROWS
            query = qr[r, b * 4 : (b + 1) * 4].reshape(QROWS, LANES).astype(F32) * 0.125
            new_bias = jnp.where(
                lax.broadcasted_iota(jnp.int32, (QROWS, keys), 1)
                <= lax.broadcasted_iota(jnp.int32, (QROWS, keys), 0) + b * QROWS,
                0.0,
                -1e30,
            )
            heads = []
            for h in range(2):
                own = low_head if h == 0 else jnp.logical_not(low_head)
                one = jnp.where(own, query, 0.0).astype(BF16)
                old = (
                    lax.dot_general(one, kbuf[:CACHE, :], NT, preferred_element_type=F32)
                    + old_bias
                )
                new = (
                    lax.dot_general(
                        one, kbuf[CACHE : CACHE + keys, :], NT, preferred_element_type=F32
                    )
                    + new_bias
                )
                top = jnp.maximum(
                    jnp.max(old, axis=1, keepdims=True), jnp.max(new, axis=1, keepdims=True)
                )
                old = jnp.exp(old - top)
                new = jnp.exp(new - top)
                total = jnp.sum(old, axis=1, keepdims=True) + jnp.sum(new, axis=1, keepdims=True)
                value = jnp.dot(
                    old.astype(BF16), vbuf[:CACHE, :], preferred_element_type=F32
                ) + jnp.dot(
                    new.astype(BF16), vbuf[CACHE : CACHE + keys, :], preferred_element_type=F32
                )
                heads.append(value / total)
            both = jnp.where(low_head, heads[0], heads[1]).astype(BF16)
            asend[b * 4 : (b + 1) * 4, r] = both.reshape(4, PER, LANES)
        att_own(r).start()
        for d in range(1, N_TOK):
            att_copy(r, d).start()
        return carry

    with jax.named_scope("attend"):
        lax.fori_loop(0, REQ, one_request, 0)

    send_own(1)
    send_own(2)
    keep_cache = pltpu.make_async_copy(cbuf, cache_out, local.at[5])
    keep_cache.start()

    for r in range(REQ):
        att_own(r).wait()
        for d in range(1, N_TOK):
            s = (me + N_TOK - d) % N_TOK
            remote(
                asend.at[s, r],
                arecv.at[pl.ds(r * PER, PER), lanes(s)],
                att_s.at[r, d],
                att_r.at[r, d],
                tok=s,
            ).wait_recv()

    with jax.named_scope("dispatch"):
        load_out.wait()
        resid[...] = states[...].astype(F32) + jnp.dot(
            arecv[...], wout[...], preferred_element_type=F32
        )
        moe_in = normed_of(resid[...], gains[1:2, :]).astype(BF16)
        both_places = (place0[...].astype(F32) + place1[...].astype(F32)).astype(BF16)
        dsend[...] = (
            jnp.dot(both_places, moe_in, preferred_element_type=F32)
            .astype(BF16)
            .reshape(N_BLK, SLOTS, D)
        )

    def disp_copy(d):
        j = (mine + d) % PEERS
        e = j % N_BLK
        return remote(
            dsend.at[e],
            drecv.at[mine],
            disp_s.at[d],
            disp_r.at[d],
            tok=mx * 2 + j // N_BLK,
            blk=e,
        )

    disp_own = pltpu.make_async_copy(dsend.at[mb], drecv.at[mine], local.at[6])
    disp_own.start()

    def start_disp(d, carry):
        disp_copy(d).start()
        return carry

    lax.fori_loop(1, PEERS, start_disp, 0)
    forward(0)

    with jax.named_scope("gates"):
        logits = lax.dot_general(router[...], moe_in, NT, preferred_element_type=F32)
        diag = lax.broadcasted_iota(jnp.int32, (TOK, TOK), 0) == lax.broadcasted_iota(
            jnp.int32, (TOK, TOK), 1
        )
        gate_cols = []
        for hot in (hot0, hot1):
            chosen = jnp.sum(jnp.where(hot > 0.5, logits, 0.0), axis=0, keepdims=True)
            gate = jax.nn.sigmoid(chosen)
            gate_cols.append(jnp.sum(jnp.where(diag, gate, 0.0), axis=1, keepdims=True))

    with jax.named_scope("fresh"):

        def pair(i, carry):
            r, s = i // 4, (i % 4) * 2
            for which in range(2):
                piece = qr[(1 + which) * REQ + r, pl.ds(s, 2)].reshape(2 * PER, LANES)
                wide[pl.ds(which, 2 * PER, stride=2), :] = piece.astype(F32)
            kv_out[pl.ds(pl.multiple_of(i * 256, 256), 256), :] = wide[:256, :].astype(BF16)
            return carry

        lax.fori_loop(0, REQ * 4, pair, 0)

    disp_own.wait()

    def wait_disp(d, carry):
        j = (mine + PEERS - d) % PEERS
        remote(
            dsend.at[j % N_BLK], drecv.at[j], disp_s.at[d], disp_r.at[d], tok=mx * 2 + 1 - mz
        ).wait_recv()
        return carry

    lax.fori_loop(1, PEERS, wait_disp, 0)

    def expert(k, i):
        first = pl.multiple_of(i * (CHUNK // SLOTS), CHUNK // SLOTS)
        rows = drecv[pl.ds(first, CHUNK // SLOTS)].reshape(CHUNK, D)
        gate = lax.dot_general(rows, wg[k, :FFS, :], NT, preferred_element_type=F32)
        up = lax.dot_general(rows, wg[k, FFS:, :], NT, preferred_element_type=F32)
        hidden = (jax.nn.gelu(gate, approximate=True) * up).astype(BF16)
        return first, jnp.dot(hidden, wd[k], preferred_element_type=F32)

    def arow(i):
        return pl.ds(pl.multiple_of(i * CHUNK, CHUNK), CHUNK)

    load_gu.wait()
    load_dn.wait()
    with jax.named_scope("expert0"):

        def first_quarter(i, carry):
            acc[arow(i), :] = expert(0, i)[1]
            return carry

        lax.fori_loop(0, PEERS * SLOTS // CHUNK, first_quarter, 0)
    forward(1)
    forward(2)
    with jax.named_scope("expert12"):

        def middle(n, carry):
            k, i = 1 + n // 4, n % 4
            acc[arow(i), :] += expert(k, i)[1]
            return carry

        lax.fori_loop(0, 2 * PEERS * SLOTS // CHUNK, middle, 0)
    for c in range(3):
        for side in range(2):
            lo = side * (FFS // 2)
            fwd_copy(c, side).wait_recv()

    def ret_copy(j):
        return remote(
            rsend.at[j],
            rrecv.at[mine],
            ret_s.at[j],
            ret_r.at[mine],
            tok=mx * 2 + j // N_BLK,
            blk=j % N_BLK,
        )

    ret_own = pltpu.make_async_copy(rsend.at[mine], rrecv.at[mine], local.at[7])
    per = CHUNK // SLOTS
    with jax.named_scope("expert3"):

        def last(n, carry):
            i = (n + mine // per) % (PEERS // per)
            first, value = expert(3, i)
            rsend[pl.ds(first, per)] = (
                (acc[arow(i), :] + value).astype(BF16).reshape(per, SLOTS, D)
            )

            def start_ret(q, inner):
                j = i * per + (q + mine) % per

                @pl.when(j == mine)
                def _():
                    ret_own.start()

                @pl.when(j != mine)
                def _():
                    ret_copy(j).start()

                return inner

            return lax.fori_loop(0, per, start_ret, carry)

        lax.fori_loop(0, PEERS // per, last, 0)

    ret_own.wait()

    def wait_ret(d, carry):
        j = (mine + d) % PEERS
        remote(rsend.at[j], rrecv.at[j], ret_s.at[j], ret_r.at[j], tok=mx * 2 + 1 - mz).wait_recv()
        return carry

    lax.fori_loop(1, PEERS, wait_ret, 0)

    with jax.named_scope("combine"):
        back = [rrecv[z * N_BLK : (z + 1) * N_BLK].reshape(N_BLK * SLOTS, D) for z in range(2)]
        total = resid[...]
        for place, gate in ((place0, gate_cols[0]), (place1, gate_cols[1])):
            picked = lax.dot_general(
                place[...], back[0], TN, preferred_element_type=F32
            ) + lax.dot_general(place[...], back[1], TN, preferred_element_type=F32)
            total = total + gate * picked
        out[...] = total.astype(BF16)

    keep_cache.wait()
    for d in range(1, N_TOK):
        qkv_copy(d).wait_send()
        for r in range(REQ):
            cache_copy(r, d).wait_send()
            att_copy(r, d).wait_send()
    for c in range(3):
        for side in range(2):
            own_copy(c, side).wait_send()
            fwd_copy(c, side).wait_send()

    def drain(d, carry):
        disp_copy(d).wait_send()
        ret_copy((mine + d) % PEERS).wait_send()
        return carry

    lax.fori_loop(1, PEERS, drain, 0)


def cache_kernel(blocks, old, fresh, out, zeros, sems):
    zeros[...] = jnp.zeros_like(zeros)
    for r in range(REQ):
        count = blocks[r]
        pltpu.make_async_copy(
            fresh.at[r],
            out.at[r, pl.ds(pl.multiple_of(count * LANES, LANES), NEW)],
            sems.at[r, 12],
        ).start()
        for j in range(12):

            @pl.when(j < count)
            def _():
                pltpu.make_async_copy(
                    old.at[r, pl.ds(j * LANES, LANES)],
                    out.at[r, pl.ds(j * LANES, LANES)],
                    sems.at[r, j],
                ).start()

            @pl.when(j >= count)
            def _():
                pltpu.make_async_copy(
                    zeros, out.at[r, pl.ds((j + 4) * LANES, LANES)], sems.at[r, j]
                ).start()

    for r in range(REQ):
        pltpu.make_async_copy(fresh.at[r], out.at[r, pl.ds(0, NEW)], sems.at[r, 12]).wait()
        for j in range(12):
            pltpu.make_async_copy(zeros, out.at[r, pl.ds(0, LANES)], sems.at[r, j]).wait()


def body(
    states,
    gain_attn,
    w_qkv,
    w_out,
    cache_prev,
    cached_blocks,
    gain_moe,
    w_router,
    routes,
    w_gate_up,
    w_down,
):
    gains = jnp.stack([gain_attn, gain_moe]).astype(F32)
    routes_rows = jnp.transpose(routes[0], (2, 0, 1)).reshape(2, TOK)
    w_gu = jnp.transpose(w_gate_up[0], (0, 2, 1)).reshape(2 * FFS, D)
    vmem = pl.BlockSpec(memory_space=pltpu.VMEM)
    hbm = pl.BlockSpec(memory_space=pl.ANY)
    smem = pl.BlockSpec(memory_space=pltpu.SMEM)
    sem = pltpu.SemaphoreType.DMA
    out, cache_out, kv_new = pl.pallas_call(
        layer_kernel,
        name="layer",
        out_shape=(
            jax.ShapeDtypeStruct((TOK, D), BF16),
            jax.ShapeDtypeStruct((REQ, N_TOK, PART, 2, LANES), BF16),
            jax.ShapeDtypeStruct((REQ * NEW * 2, LANES), BF16),
        ),
        in_specs=[smem, vmem, vmem, vmem, vmem, hbm, hbm, hbm, hbm, hbm],
        out_specs=(vmem, hbm, vmem),
        scratch_shapes=[
            pltpu.VMEM((D, 3 * D), BF16),
            pltpu.VMEM((D, D), BF16),
            pltpu.VMEM((REQ, N_TOK, PART, 2, LANES), BF16),
            pltpu.VMEM((N_TOK, 3 * REQ, PER, LANES), BF16),
            pltpu.VMEM((3 * REQ, N_TOK, PER, LANES), BF16),
            pltpu.VMEM((CACHE + NEW, LANES), BF16),
            pltpu.VMEM((CACHE + NEW, LANES), BF16),
            pltpu.VMEM((2 * PART, LANES), F32),
            pltpu.VMEM((N_TOK, REQ, PER, LANES), BF16),
            pltpu.VMEM((TOK, D), BF16),
            pltpu.VMEM((TOK, D), F32),
            pltpu.VMEM((N_BLK * SLOTS, TOK), BF16),
            pltpu.VMEM((N_BLK * SLOTS, TOK), BF16),
            pltpu.VMEM((N_BLK, SLOTS, D), BF16),
            pltpu.VMEM((PEERS, SLOTS, D), BF16),
            pltpu.VMEM((4, 2 * FFS, D), BF16),
            pltpu.VMEM((4, FFS, D), BF16),
            pltpu.VMEM((PEERS * SLOTS, D), F32),
            pltpu.VMEM((PEERS, SLOTS, D), BF16),
            pltpu.VMEM((PEERS, SLOTS, D), BF16),
            sem((8,)),
            sem((REQ, N_TOK)),
            sem((REQ, N_TOK)),
            sem((REQ,)),
            sem((N_TOK,)),
            sem((N_TOK,)),
            sem((REQ, N_TOK)),
            sem((REQ, N_TOK)),
            sem((REQ,)),
            sem((3, 2)),
            sem((3, 2)),
            sem((3, 2)),
            sem((3, 2)),
            sem((PEERS,)),
            sem((PEERS,)),
            sem((PEERS,)),
            sem((PEERS,)),
        ],
        compiler_params=pltpu.CompilerParams(
            collective_id=0, has_side_effects=True, vmem_limit_bytes=60 * 1024 * 1024
        ),
    )(
        cached_blocks,
        states.reshape(TOK, D),
        gains,
        routes_rows,
        jnp.transpose(w_router),
        w_qkv,
        w_out,
        cache_prev,
        w_gu,
        w_down[0],
    )
    decode_cache = pl.pallas_call(
        cache_kernel,
        name="place_cache",
        out_shape=jax.ShapeDtypeStruct((REQ, CACHE + NEW, 2, LANES), BF16),
        in_specs=[smem, vmem, vmem],
        out_specs=hbm,
        scratch_shapes=[pltpu.VMEM((LANES, 2, LANES), BF16), sem((REQ, 13))],
    )(
        cached_blocks,
        cache_out.reshape(REQ, CACHE, 2, LANES),
        kv_new.reshape(REQ, NEW, 2, LANES),
    )
    return (out.reshape(REQ, PER, D), decode_cache)


def solution(mesh):
    return jax.shard_map(
        body,
        mesh=mesh,
        in_specs=(
            P("blk", "tok", None),
            P(),
            P(),
            P(),
            P("blk", "tok", None, None),
            P("blk"),
            P(),
            P(),
            P("tok", "blk", None, None),
            P("blk", None, None, "tok"),
            P("blk", "tok", None),
        ),
        out_specs=(P("blk", "tok", None), P("blk", None, None, "tok")),
        check_vma=False,
    )
```

```python
import jax
import jax.numpy as jnp
from jax import lax
from jax.experimental import pallas as pl
from jax.experimental.pallas import tpu as pltpu
from jax.sharding import PartitionSpec as P

MESH = pl.DeviceIdType.MESH
F32, BF16 = jnp.float32, jnp.bfloat16
NT = (((1,), (1,)), ((), ()))
TN = (((0,), (0,)), ((), ()))
REQ, PER, D = 3, 64, 1024
TOK = REQ * PER
N_TOK, N_BLK, N_X = 8, 16, 4
PEERS = 2 * N_BLK
SLOTS = 32
CACHE, NEW = 1536, 512
PART = CACHE // N_TOK
FFS = 352
QROWS = 256
TOK_ORDER = ((1, 1), (3, 0), (3, 1), (1, 0), (2, 1), (2, 0), (0, 1))
PLANES = ((0, 0), (1, 0), (1, 1), (0, 1))
EXP_ORDER = tuple(
    (*PLANES[i], (1, 0, 3, 2)[(k + i) % 4], c)
    for c in range(2)
    for k in range(4)
    for i in range(4)
    if (*PLANES[i], (1, 0, 3, 2)[(k + i) % 4], c) != (0, 0, 0, 0)
)
CHUNK = 256
LANES = 128


def normed_of(values, gain):
    return values * lax.rsqrt(jnp.mean(values * values, -1, keepdims=True) + 1e-06) * gain


def layer_kernel(
    blocks,
    states,
    gain_a,
    gain_m,
    routes,
    router,
    w_qkv,
    w_out,
    cache,
    w_gu,
    w_dn,
    out,
    cache_out,
    kv_out,
    wqkv,
    wout,
    cbuf,
    qs,
    qr,
    kbuf,
    vbuf,
    wide,
    asend,
    arecv,
    resid,
    place0,
    place1,
    dsend,
    drecv,
    wg,
    wd,
    acc,
    rsend,
    rrecv,
    hid,
    local,
    cache_s,
    cache_r,
    cache_l,
    qkv_s,
    qkv_r,
    att_s,
    att_r,
    att_l,
    own_s,
    own_r,
    fwd_s,
    fwd_r,
    disp_s,
    disp_r,
    ret_s,
    ret_r,
):
    me = lax.axis_index("tok")
    mb = lax.axis_index("blk")
    mx, mz = me // 2, me % 2
    mine = mz * N_BLK + mb
    right = ((mx + 1) % N_X) * 2 + mz
    left = ((mx + N_X - 1) % N_X) * 2 + mz
    far_z, my, core = mb // 8, (mb // 2) % 4, mb % 2

    def peer(i, way):
        dx, dz = TOK_ORDER[i]
        return ((mx + way * dx + N_X) % N_X) * 2 + (mz + dz) % 2

    def pair_of(i, way):
        dz, dfar, dy, dc = EXP_ORDER[i]
        y = (my + way * dy + 4) % 4
        return {
            "tok": mx * 2 + (mz + dz) % 2,
            "blk": (((far_z + dfar) % 2) * 4 + y) * 2 + (core + dc) % 2,
        }

    def remote(src, dst, ssem, rsem, **where):
        return pltpu.make_async_remote_copy(
            src_ref=src,
            dst_ref=dst,
            send_sem=ssem,
            recv_sem=rsem,
            device_id=where,
            device_id_type=MESH,
        )

    def lanes(t):
        return pl.ds(pl.multiple_of(t * LANES, LANES), LANES)

    barrier = pltpu.get_barrier_semaphore()
    for i in range(N_TOK - 1):
        pl.semaphore_signal(
            barrier, inc=1, device_id={"tok": peer(i, 1)}, device_id_type=MESH
        )
    for i in range(PEERS - 1):
        pl.semaphore_signal(barrier, inc=1, device_id=pair_of(i, 1), device_id_type=MESH)

    load_qkv = [
        pltpu.make_async_copy(
            w_qkv.at[pl.ds(q * 256, 256)], wqkv.at[pl.ds(q * 256, 256)], local.at[8 + q]
        )
        for q in range(4)
    ]
    load_out = pltpu.make_async_copy(w_out, wout, local.at[1])
    load_gu = pltpu.make_async_copy(w_gu, wg.at[0], local.at[2])
    load_dn = pltpu.make_async_copy(w_dn, wd.at[0], local.at[3])
    for part in load_qkv:
        part.start()
    pl.semaphore_wait(barrier, N_TOK - 1 + PEERS - 1)

    def cache_copy(r, d):
        t = peer(d - 1, 1)
        return remote(
            cache.at[r, :, :, lanes(t)],
            cbuf.at[r, me],
            cache_s.at[r, d],
            cache_r.at[r, d],
            tok=t,
        )

    def cache_own(r):
        return pltpu.make_async_copy(cache.at[r, :, :, lanes(me)], cbuf.at[r, me], cache_l.at[r])

    def send_cache(r):
        cache_own(r).start()
        for d in range(1, N_TOK):
            cache_copy(r, d).start()

    send_cache(0)
    send_cache(1)
    load_out.start()
    load_gu.start()
    load_dn.start()

    with jax.named_scope("project"):
        flat = states[...].astype(F32)
        normed = normed_of(flat, gain_a[...].astype(F32).reshape(1, D)).astype(BF16)
        for part in load_qkv:
            part.wait()
        for c in range(12):
            part = jnp.dot(
                normed, wqkv[:, c * 256 : (c + 1) * 256], preferred_element_type=F32
            ).astype(BF16)
            j, t = c // 4, (c % 4) * 2
            for half in range(2):
                qs[t + half, j * REQ : (j + 1) * REQ] = part[
                    :, half * LANES : (half + 1) * LANES
                ].reshape(REQ, PER, LANES)

    def qkv_copy(d):
        t = peer(d - 1, 1)
        return remote(qs.at[t], qr.at[:, me], qkv_s.at[d], qkv_r.at[d], tok=t)

    qkv_own = pltpu.make_async_copy(qs.at[me], qr.at[:, me], local.at[4])
    qkv_own.start()
    for d in range(1, N_TOK):
        qkv_copy(d).start()
    send_cache(2)

    def chunk_of(ref_g, ref_d, c, lo, rows):
        if c < 2:
            return ref_g.at[pl.ds(c * FFS + lo, rows)]
        return ref_d.at[pl.ds(lo, rows)]

    def own_copy(c, side):
        return remote(
            chunk_of(w_gu, w_dn, c, 0, FFS),
            chunk_of(wg.at[1 + side], wd.at[1 + side], c, 0, FFS),
            own_s.at[c, side],
            own_r.at[c, side],
            tok=right if side == 0 else left,
        )

    def fwd_copy(c, side):
        lo = side * (FFS // 2)
        return remote(
            chunk_of(wg.at[1 + side], wd.at[1 + side], c, lo, FFS // 2),
            chunk_of(wg.at[3], wd.at[3], c, lo, FFS // 2),
            fwd_s.at[c, side],
            fwd_r.at[c, side],
            tok=right if side == 0 else left,
        )

    def send_own(c):
        for side in range(2):
            own_copy(c, side).start()

    def forward(c):
        for side in range(2):
            own_copy(c, side).wait_recv()
            fwd_copy(c, side).start()

    send_own(0)

    with jax.named_scope("places"):
        picks = jnp.concatenate([routes[r] for r in range(REQ)], axis=1)
        r0, r1 = picks[0:1, :], picks[1:2, :]
        expert = lax.broadcasted_iota(jnp.int32, (N_BLK, TOK), 0)
        hot0 = (expert == r0).astype(F32)
        hot1 = (expert == r1).astype(F32)
        earlier = (
            lax.broadcasted_iota(jnp.int32, (TOK, TOK), 0)
            < lax.broadcasted_iota(jnp.int32, (TOK, TOK), 1)
        ).astype(BF16)
        before0 = jnp.dot(hot0.astype(BF16), earlier, preferred_element_type=F32)
        before1 = jnp.dot(hot1.astype(BF16), earlier, preferred_element_type=F32)
        before1 = before1 + jnp.sum(hot0, axis=1, keepdims=True)
        rank0 = jnp.sum(before0 * hot0, axis=0, keepdims=True).astype(jnp.int32)
        rank1 = jnp.sum(before1 * hot1, axis=0, keepdims=True).astype(jnp.int32)
        slot = lax.broadcasted_iota(jnp.int32, (N_BLK * SLOTS, TOK), 0)
        place0[...] = (slot == r0 * SLOTS + rank0).astype(F32).astype(BF16)
        place1[...] = (slot == r1 * SLOTS + rank1).astype(F32).astype(BF16)

    qkv_own.wait()
    for d in range(1, N_TOK):
        s = peer(d - 1, -1)
        remote(qs.at[s], qr.at[:, s], qkv_s.at[d], qkv_r.at[d], tok=s).wait_recv()

    low_head = lax.broadcasted_iota(jnp.int32, (QROWS, LANES), 1) < LANES // 2

    def att_copy(r, d):
        t = peer(d - 1, 1)
        return remote(
            asend.at[t, r],
            arecv.at[pl.ds(pl.multiple_of(r * PER, PER), PER), lanes(me)],
            att_s.at[r, d],
            att_r.at[r, d],
            tok=t,
        )

    def att_own(r):
        return pltpu.make_async_copy(
            asend.at[me, r],
            arecv.at[pl.ds(pl.multiple_of(r * PER, PER), PER), lanes(me)],
            att_l.at[r],
        )

    def one_request(r, carry):
        cache_own(r).wait()
        for d in range(1, N_TOK):
            s = peer(d - 1, -1)
            remote(
                cache.at[r, :, :, lanes(s)], cbuf.at[r, s], cache_s.at[r, d], cache_r.at[r, d], tok=s
            ).wait_recv()

        def split(s, inner):
            wide[...] = cbuf.at[r, s].reshape(2 * PART, LANES)[...].astype(F32)
            rows = pl.ds(pl.multiple_of(s * PART, PART), PART)
            kbuf[rows, :] = wide[pl.ds(0, PART, stride=2), :].astype(BF16)
            vbuf[rows, :] = wide[pl.ds(1, PART, stride=2), :].astype(BF16)
            return inner

        lax.fori_loop(0, N_TOK, split, 0)
        kbuf[CACHE:, :] = qr[REQ + r].reshape(NEW, LANES)
        vbuf[CACHE:, :] = qr[2 * REQ + r].reshape(NEW, LANES)
        length = blocks[r] * LANES
        old_bias = jnp.where(
            lax.broadcasted_iota(jnp.int32, (1, CACHE), 1) < length, 0.0, -1e30
        )
        for b in range(NEW // QROWS):
            keys = (b + 1) * QROWS
            query = qr[r, b * 4 : (b + 1) * 4].reshape(QROWS, LANES).astype(F32) * 0.125
            new_bias = jnp.where(
                lax.broadcasted_iota(jnp.int32, (QROWS, keys), 1)
                <= lax.broadcasted_iota(jnp.int32, (QROWS, keys), 0) + b * QROWS,
                0.0,
                -1e30,
            )
            heads = []
            for h in range(2):
                own = low_head if h == 0 else jnp.logical_not(low_head)
                one = jnp.where(own, query, 0.0).astype(BF16)
                old = (
                    lax.dot_general(one, kbuf[:CACHE, :], NT, preferred_element_type=F32)
                    + old_bias
                )
                new = (
                    lax.dot_general(
                        one, kbuf[CACHE : CACHE + keys, :], NT, preferred_element_type=F32
                    )
                    + new_bias
                )
                top = jnp.maximum(
                    jnp.max(old, axis=1, keepdims=True), jnp.max(new, axis=1, keepdims=True)
                )
                old = jnp.exp(old - top)
                new = jnp.exp(new - top)
                total = jnp.sum(old, axis=1, keepdims=True) + jnp.sum(new, axis=1, keepdims=True)
                value = jnp.dot(
                    old.astype(BF16), vbuf[:CACHE, :], preferred_element_type=F32
                ) + jnp.dot(
                    new.astype(BF16), vbuf[CACHE : CACHE + keys, :], preferred_element_type=F32
                )
                heads.append(value / total)
            both = jnp.where(low_head, heads[0], heads[1]).astype(BF16)
            asend[b * 4 : (b + 1) * 4, r] = both.reshape(4, PER, LANES)
        att_own(r).start()
        for d in range(1, N_TOK):
            att_copy(r, d).start()
        return carry

    with jax.named_scope("attend"):
        lax.fori_loop(0, REQ, one_request, 0)

    send_own(1)
    send_own(2)
    keep_cache = pltpu.make_async_copy(cbuf, cache_out, local.at[5])
    keep_cache.start()

    for r in range(REQ):
        att_own(r).wait()
        for d in range(1, N_TOK):
            s = peer(d - 1, -1)
            remote(
                asend.at[s, r],
                arecv.at[pl.ds(r * PER, PER), lanes(s)],
                att_s.at[r, d],
                att_r.at[r, d],
                tok=s,
            ).wait_recv()

    with jax.named_scope("dispatch"):
        load_out.wait()
        resid[...] = states[...].astype(F32) + jnp.dot(
            arecv[...], wout[...], preferred_element_type=F32
        )
        moe_in = normed_of(resid[...], gain_m[...].astype(F32).reshape(1, D)).astype(BF16)
        both_places = (place0[...].astype(F32) + place1[...].astype(F32)).astype(BF16)
        dsend[...] = (
            jnp.dot(both_places, moe_in, preferred_element_type=F32)
            .astype(BF16)
            .reshape(N_BLK, SLOTS, D)
        )

    def disp_copy(i):
        to = pair_of(i, 1)
        return remote(dsend.at[to["blk"]], drecv.at[i], disp_s.at[i], disp_r.at[i], **to)

    disp_own = pltpu.make_async_copy(dsend.at[mb], drecv.at[PEERS - 1], local.at[6])
    for i in range(PEERS - 1):
        disp_copy(i).start()
    disp_own.start()
    forward(0)

    with jax.named_scope("gates"):
        logits = lax.dot_general(router[...], moe_in, NT, preferred_element_type=F32)
        diag = lax.broadcasted_iota(jnp.int32, (TOK, TOK), 0) == lax.broadcasted_iota(
            jnp.int32, (TOK, TOK), 1
        )
        gate_cols = []
        for hot in (hot0, hot1):
            chosen = jnp.sum(jnp.where(hot > 0.5, logits, 0.0), axis=0, keepdims=True)
            gate = jax.nn.sigmoid(chosen)
            gate_cols.append(jnp.sum(jnp.where(diag, gate, 0.0), axis=1, keepdims=True))

    with jax.named_scope("fresh"):

        def pair(i, carry):
            r, s = i // 4, (i % 4) * 2
            for which in range(2):
                piece = qr[(1 + which) * REQ + r, pl.ds(s, 2)].reshape(2 * PER, LANES)
                wide[pl.ds(which, 2 * PER, stride=2), :] = piece.astype(F32)
            kv_out[pl.ds(pl.multiple_of(i * 256, 256), 256), :] = wide[:256, :].astype(BF16)
            return carry

        lax.fori_loop(0, REQ * 4, pair, 0)

    forward(1)
    disp_own.wait()
    for i in range(PEERS - 1):
        disp_copy(i).wait_recv()

    def hidden_of(k, i):
        first = pl.multiple_of(i * (CHUNK // SLOTS), CHUNK // SLOTS)
        rows = drecv[pl.ds(first, CHUNK // SLOTS)].reshape(CHUNK, D)
        gate = lax.dot_general(rows, wg[k, :FFS, :], NT, preferred_element_type=F32)
        up = lax.dot_general(rows, wg[k, FFS:, :], NT, preferred_element_type=F32)
        return (jax.nn.gelu(gate, approximate=True) * up).astype(BF16)

    def expert(k, i):
        return jnp.dot(hidden_of(k, i), wd[k], preferred_element_type=F32)

    def arow(i):
        return pl.ds(pl.multiple_of(i * CHUNK, CHUNK), CHUNK)

    load_gu.wait()
    load_dn.wait()
    with jax.named_scope("expert0"):

        def first_quarter(i, carry):
            acc[arow(i), :] = expert(0, i)
            return carry

        lax.fori_loop(0, PEERS * SLOTS // CHUNK, first_quarter, 0)
    forward(2)
    with jax.named_scope("expert12"):

        def middle(n, carry):
            k, i = 1 + n // 4, n % 4
            acc[arow(i), :] += expert(k, i)
            return carry

        lax.fori_loop(0, 2 * PEERS * SLOTS // CHUNK, middle, 0)
    for c in range(2):
        for side in range(2):
            fwd_copy(c, side).wait_recv()
    with jax.named_scope("hidden3"):

        def last_hidden(i, carry):
            hid[arow(i), :] = hidden_of(3, i)
            return carry

        lax.fori_loop(0, PEERS * SLOTS // CHUNK, last_hidden, 0)
    for side in range(2):
        fwd_copy(2, side).wait_recv()

    def ret_copy(i):
        return remote(
            rsend.at[i], rrecv.at[mine], ret_s.at[i], ret_r.at[i], **pair_of(i, -1)
        )

    ret_own = pltpu.make_async_copy(rsend.at[PEERS - 1], rrecv.at[mine], local.at[7])
    per = CHUNK // SLOTS
    with jax.named_scope("expert3"):
        for n in range(PEERS // per):
            here = slice(n * CHUNK, (n + 1) * CHUNK)
            value = acc[here, :] + jnp.dot(hid[here, :], wd[3], preferred_element_type=F32)
            rsend[n * per : (n + 1) * per] = value.astype(BF16).reshape(per, SLOTS, D)
            for i in range(n * per, (n + 1) * per):
                if i == PEERS - 1:
                    ret_own.start()
                else:
                    ret_copy(i).start()

    ret_own.wait()
    for i in range(PEERS - 1):
        at = pair_of(i, 1)
        remote(
            rsend.at[i],
            rrecv.at[((mz + EXP_ORDER[i][0]) % 2) * N_BLK + at["blk"]],
            ret_s.at[i],
            ret_r.at[i],
            **at,
        ).wait_recv()

    with jax.named_scope("combine"):
        back = [rrecv[z * N_BLK : (z + 1) * N_BLK].reshape(N_BLK * SLOTS, D) for z in range(2)]
        total = resid[...]
        for place, gate in ((place0, gate_cols[0]), (place1, gate_cols[1])):
            picked = lax.dot_general(
                place[...], back[0], TN, preferred_element_type=F32
            ) + lax.dot_general(place[...], back[1], TN, preferred_element_type=F32)
            total = total + gate * picked
        out[...] = total.astype(BF16)

    keep_cache.wait()
    for d in range(1, N_TOK):
        qkv_copy(d).wait_send()
        for r in range(REQ):
            cache_copy(r, d).wait_send()
            att_copy(r, d).wait_send()
    for c in range(3):
        for side in range(2):
            own_copy(c, side).wait_send()
            fwd_copy(c, side).wait_send()

    for i in range(PEERS - 1):
        disp_copy(i).wait_send()
        ret_copy(i).wait_send()


def cache_kernel(blocks, old, fresh, out, old_v, fresh_v, zeros, load, sems):
    loads = [
        (
            pltpu.make_async_copy(old.at[r], old_v.at[r], load.at[r, 0]),
            pltpu.make_async_copy(fresh.at[r], fresh_v.at[r], load.at[r, 1]),
        )
        for r in range(REQ)
    ]
    for pair in loads:
        for copy in pair:
            copy.start()
    zeros[...] = jnp.zeros_like(zeros)
    for r in range(REQ):
        count = blocks[r]
        for j in range(12):

            @pl.when(j >= count)
            def _():
                pltpu.make_async_copy(
                    zeros, out.at[r, pl.ds((j + 4) * LANES, LANES)], sems.at[r, j]
                ).start()

    for r in range(REQ):
        count = blocks[r]
        for copy in loads[r]:
            copy.wait()
        pltpu.make_async_copy(
            fresh_v.at[r],
            out.at[r, pl.ds(pl.multiple_of(count * LANES, LANES), NEW)],
            sems.at[r, 12],
        ).start()
        for j in range(12):

            @pl.when(j < count)
            def _():
                pltpu.make_async_copy(
                    old_v.at[r, pl.ds(j * LANES, LANES)],
                    out.at[r, pl.ds(j * LANES, LANES)],
                    sems.at[r, j],
                ).start()

    for r in range(REQ):
        pltpu.make_async_copy(fresh_v.at[r], out.at[r, pl.ds(0, NEW)], sems.at[r, 12]).wait()
        for j in range(12):
            pltpu.make_async_copy(zeros, out.at[r, pl.ds(0, LANES)], sems.at[r, j]).wait()


def body(
    states,
    gain_attn,
    w_qkv,
    w_out,
    cache_prev,
    cached_blocks,
    gain_moe,
    w_router,
    routes,
    w_gate_up,
    w_down,
):
    routes_rows = jnp.transpose(routes[0], (0, 2, 1))
    w_gu = jnp.transpose(w_gate_up[0], (0, 2, 1)).reshape(2 * FFS, D)
    vmem = pl.BlockSpec(memory_space=pltpu.VMEM)
    hbm = pl.BlockSpec(memory_space=pl.ANY)
    smem = pl.BlockSpec(memory_space=pltpu.SMEM)
    sem = pltpu.SemaphoreType.DMA
    out, cache_out, kv_new = pl.pallas_call(
        layer_kernel,
        name="layer",
        out_shape=(
            jax.ShapeDtypeStruct((TOK, D), BF16),
            jax.ShapeDtypeStruct((REQ, N_TOK, PART, 2, LANES), BF16),
            jax.ShapeDtypeStruct((REQ * NEW * 2, LANES), BF16),
        ),
        in_specs=[smem, vmem, vmem, vmem, vmem, vmem, hbm, hbm, hbm, hbm, hbm],
        out_specs=(vmem, hbm, vmem),
        scratch_shapes=[
            pltpu.VMEM((D, 3 * D), BF16),
            pltpu.VMEM((D, D), BF16),
            pltpu.VMEM((REQ, N_TOK, PART, 2, LANES), BF16),
            pltpu.VMEM((N_TOK, 3 * REQ, PER, LANES), BF16),
            pltpu.VMEM((3 * REQ, N_TOK, PER, LANES), BF16),
            pltpu.VMEM((CACHE + NEW, LANES), BF16),
            pltpu.VMEM((CACHE + NEW, LANES), BF16),
            pltpu.VMEM((2 * PART, LANES), F32),
            pltpu.VMEM((N_TOK, REQ, PER, LANES), BF16),
            pltpu.VMEM((TOK, D), BF16),
            pltpu.VMEM((TOK, D), F32),
            pltpu.VMEM((N_BLK * SLOTS, TOK), BF16),
            pltpu.VMEM((N_BLK * SLOTS, TOK), BF16),
            pltpu.VMEM((N_BLK, SLOTS, D), BF16),
            pltpu.VMEM((PEERS, SLOTS, D), BF16),
            pltpu.VMEM((4, 2 * FFS, D), BF16),
            pltpu.VMEM((4, FFS, D), BF16),
            pltpu.VMEM((PEERS * SLOTS, D), F32),
            pltpu.VMEM((PEERS, SLOTS, D), BF16),
            pltpu.VMEM((PEERS, SLOTS, D), BF16),
            pltpu.VMEM((PEERS * SLOTS, FFS), BF16),
            sem((12,)),
            sem((REQ, N_TOK)),
            sem((REQ, N_TOK)),
            sem((REQ,)),
            sem((N_TOK,)),
            sem((N_TOK,)),
            sem((REQ, N_TOK)),
            sem((REQ, N_TOK)),
            sem((REQ,)),
            sem((3, 2)),
            sem((3, 2)),
            sem((3, 2)),
            sem((3, 2)),
            sem((PEERS,)),
            sem((PEERS,)),
            sem((PEERS,)),
            sem((PEERS,)),
        ],
        compiler_params=pltpu.CompilerParams(
            collective_id=0, has_side_effects=True, vmem_limit_bytes=60 * 1024 * 1024
        ),
    )(
        cached_blocks,
        states.reshape(TOK, D),
        gain_attn,
        gain_moe,
        routes_rows,
        jnp.transpose(w_router),
        w_qkv,
        w_out,
        cache_prev,
        w_gu,
        w_down[0],
    )
    decode_cache = pl.pallas_call(
        cache_kernel,
        name="place_cache",
        out_shape=jax.ShapeDtypeStruct((REQ, CACHE + NEW, 2, LANES), BF16),
        in_specs=[smem, hbm, hbm],
        out_specs=hbm,
        scratch_shapes=[
            pltpu.VMEM((REQ, CACHE, 2, LANES), BF16),
            pltpu.VMEM((REQ, NEW, 2, LANES), BF16),
            pltpu.VMEM((LANES, 2, LANES), BF16),
            sem((REQ, 2)),
            sem((REQ, 13)),
        ],
    )(
        cached_blocks,
        cache_out.reshape(REQ, CACHE, 2, LANES),
        kv_new.reshape(REQ, NEW, 2, LANES),
    )
    return (out.reshape(REQ, PER, D), decode_cache)


def solution(mesh):
    return jax.shard_map(
        body,
        mesh=mesh,
        in_specs=(
            P("blk", "tok", None),
            P(),
            P(),
            P(),
            P("blk", "tok", None, None),
            P("blk"),
            P(),
            P(),
            P("tok", "blk", None, None),
            P("blk", None, None, "tok"),
            P("blk", "tok", None),
        ),
        out_specs=(P("blk", "tok", None), P("blk", None, None, "tok")),
        check_vma=False,
    )
```
